32 devices in a mesh: groups: 2 (over y), ep: 8 (over z, x), tp: 2 (over core).
Axes of the slice: x: 2, y: 2, z: 4, core: 2. Of those that a mesh axis runs over, the one named last changes fastest.
Arguments:
- tokens: bfloat16 [1024, 2880], P(('groups', 'ep'), 'tp'), parts along dimension 0, may hold values from -6 to 6
- expert_ids: int32 [1024, 4], P(('groups', 'ep')), parts along dimension 0, may hold values from 0 to 7, all different within a row; in each aligned block of 64 rows (0 to 63, 64 to 127, ...) at most 48 rows name the same one
- gate_probs: float32 [1024, 4], P(('groups', 'ep')), parts along dimension 0, may hold values from 0.05 to 1
- w_gate: bfloat16 [8, 2880, 1440], P('ep', None, 'tp'), may hold values from -0.109375 to 0.109375
- w_up: bfloat16 [8, 2880, 1440], P('ep', None, 'tp'), may hold values from -0.109375 to 0.109375
- w_down: bfloat16 [8, 1440, 2880], P('ep', 'tp'), may hold values from -0.15625 to 0.15625
Outputs:
- mixed: bfloat16 [1024, 2880], P(('groups', 'ep'), 'tp'), parts along dimension 0
The draws below stay inside these ranges and needn't reach their ends.
There are 2 independent parts, one for each index of `groups`. The reference program is written for one: setup_inputs(seed, part) draws one part's arguments, and reference() takes and returns one part's arrays. A program takes and returns all parts, laid end to end along the dimension named above; an argument that names none is the same for every part. Nothing has to cross between parts.
Inputs may be any that keep to these rules, and one draw needn't show every extreme that they name: `expert_ids`: within each block of 64 rows that one index of ep holds, no expert is named by more than 48 rows, and in every draw some expert is named by exactly 48 rows of some block; the numbers of one row differ.
All inputs are finite; a program needn't handle non-finite values.
Results may differ from the reference program's by a relative error of at most 0.0058.
Values may be sent and summed in bfloat16 or wider, within the bound.
A program may use at most 128 MiB of HBM per device.

```python
import math
import jax
import jax.numpy as jnp
import numpy as np
from jax import lax

D = 2880
FF = 1440
TOP = 4
TOK_EP = 64
EXPERTS = 8
TOKENS = 512
CAP_SRC = 48
N_EP = 8


def level_of(own_key, dims, split, smallest, largest):
    level = 1.0
    for position, parts in split:
        steps = jax.random.uniform(jax.random.fold_in(jax.random.fold_in(own_key, 6), position), (parts,), jnp.float32, smallest / len(split), largest / len(split))
        level = level * jnp.repeat(jnp.exp(steps), dims[position] // parts).reshape((-1,) + (1,) * (len(dims) - 1 - position))
    return level


def deal_out(own_key, own, number, rows, amount, top, limit, skew):
    sequence = jax.random.permutation(own_key, amount)
    crowded, common = load_shares(amount, rows * top, limit, skew, True), load_shares(amount, rows * top, limit, skew, False)
    places = jnp.arange(amount)

    def named(tallies, rotation):
        used = int((tallies > 0).sum())
        fixed = max(1, used // 4)
        moved = fixed + (places - fixed + rotation * (used - fixed)) % max(1, amount - fixed)
        return jnp.zeros((amount,), jnp.int32).at[sequence[jnp.where(places < fixed, places, moved)]].set(jnp.asarray(tallies, jnp.int32))

    tallies = jnp.where(number % 4 == 0, named(crowded, number // 4), named(common, number - number // 4 - 1))
    mixed = jax.random.permutation(jax.random.fold_in(own, 3), amount)
    donor, taker = mixed[0:amount // 2 * 2:2], mixed[1:amount // 2 * 2:2]
    slack = jnp.minimum(tallies[donor] - 1, limit - tallies[taker]) // 2
    slack = jnp.where((donor == sequence[0]) | (taker == sequence[0]) | (tallies[taker] == 0), 0, jnp.maximum(slack, 0))
    moved = jax.random.randint(jax.random.fold_in(own, 4), (amount // 2,), 0, 1 << 20) % (slack + 1)
    tallies = tallies.at[donor].add(-moved).at[taker].add(moved)
    labels = jnp.searchsorted(jnp.cumsum(tallies), jnp.arange(rows * top), side="right").astype(jnp.int32)
    listing = labels.reshape(top, rows).T
    listing = listing[jax.random.permutation(jax.random.fold_in(own, 1), rows)]
    rotation = jax.random.randint(jax.random.fold_in(own, 2), (rows, 1), 0, top)
    return jnp.take_along_axis(listing, (jnp.arange(top)[None, :] + rotation) % top, axis=1)


def load_shares(amount, total, bound, slope, full):
    portions = [(1 << 20) // math.isqrt(grade ** slope) + 1 for grade in range(1, amount + 1)]
    largest = bound if full else min(bound, max(-(-total // amount), total * portions[0] // sum(portions)))
    least = 1 if total - largest >= amount - 1 else 0
    holding, surplus = [largest] + [least] * (amount - 1), total - largest - least * (amount - 1)
    while surplus > 0:
        candidates = [i for i in range(1, amount) if holding[i] < largest] or [i for i in range(1, amount) if holding[i] < bound]
        whole, left = sum([portions[i] for i in candidates]), surplus
        for i in candidates:
            addition = min(bound - holding[i], max(1, left * portions[i] // whole), surplus)
            holding[i] = holding[i] + addition
            surplus = surplus - addition
    return np.array(holding)


def noise(rng, extent, scale, most, pieces=(), kind=jnp.bfloat16):
    drawn = scale * jax.random.normal(rng, extent, jnp.float32)
    if pieces:
        drawn = drawn * level_of(rng, extent, pieces, -0.22, 0.18)
    return jnp.clip(drawn, -most, most).astype(kind)


def setup_inputs(seed: int = 0, part: int = 0) -> dict:
    streams_of = jax.random.split(jax.random.key(seed), 7)
    part_splits = jax.random.split(jax.random.fold_in(streams_of[6], part), 7)
    tokens = noise(part_splits[0], (TOKENS, D), 1.0, 6.0, ((0, 8), (1, 2)))
    expert_ids_keys = jax.random.split(jax.random.fold_in(part_splits[1], 1), TOKENS // TOK_EP)
    expert_ids_turns = jax.random.permutation(jax.random.fold_in(part_splits[1], 3), TOKENS // TOK_EP)
    expert_ids = jax.vmap(lambda own, number: deal_out(jax.random.fold_in(part_splits[1], 2), own, number, TOK_EP, EXPERTS, TOP, CAP_SRC, 2))(expert_ids_keys, expert_ids_turns).reshape((TOKENS, TOP))
    gate_probs = jnp.clip(jnp.exp(math.log(1.0) - 2.9957323 * jax.random.uniform(part_splits[2], (TOKENS, TOP), jnp.float32) ** level_of(part_splits[2], (TOKENS, TOP), ((0, 8),), -0.2, 0.2)), 0.05, 1.0)
    w_gate = noise(streams_of[3], (EXPERTS, D, FF), D ** -0.5, 0.109375, ((0, 8), (2, 2)))
    w_up = noise(streams_of[4], (EXPERTS, D, FF), D ** -0.5, 0.109375, ((0, 8), (2, 2)))
    w_down = noise(streams_of[5], (EXPERTS, FF, D), FF ** -0.5, 0.15625, ((0, 8), (1, 2)))
    return {"tokens": tokens, "expert_ids": expert_ids, "gate_probs": gate_probs, "w_gate": w_gate, "w_up": w_up, "w_down": w_down}


def reference(tokens, expert_ids, gate_probs, w_gate, w_up, w_down):
    n_experts = w_gate.shape[0]
    routed = expert_ids.reshape(N_EP, TOK_EP * TOP)
    onehot = (routed[:, :, None] == jnp.arange(n_experts, dtype=jnp.int32)[None, None, :]).astype(jnp.int32)
    before = jnp.cumsum(onehot, axis=1) - onehot
    slots = jnp.sum(before * onehot, axis=2).astype(jnp.int32)
    source = jnp.arange(N_EP, dtype=jnp.int32)[:, None]
    positions = ((routed * N_EP + source) * CAP_SRC + slots).astype(jnp.int32).reshape(TOKENS * TOP)
    pair_token = jnp.repeat(jnp.arange(TOKENS, dtype=jnp.int32), TOP)
    owners = jnp.full((n_experts * N_EP * CAP_SRC,), TOKENS, jnp.int32).at[positions].set(pair_token)
    padded = jnp.concatenate([tokens, jnp.zeros((1, D), tokens.dtype)], 0)

    def expert_output(packed):
        row_index, gate_part, up_part, down_part = packed
        rows = padded[row_index]
        gated = jnp.dot(rows, gate_part, preferred_element_type=jnp.float32)
        lifted = jnp.dot(rows, up_part, preferred_element_type=jnp.float32)
        hidden = (jax.nn.silu(gated) * lifted).astype(jnp.bfloat16)
        return jnp.dot(hidden, down_part, preferred_element_type=jnp.float32).astype(jnp.bfloat16)

    outputs = lax.map(expert_output, (owners.reshape(n_experts, N_EP * CAP_SRC), w_gate, w_up, w_down))
    outputs = outputs.reshape(n_experts * N_EP * CAP_SRC, D)
    chosen = positions.reshape(TOKENS, TOP)
    mixed = jnp.zeros((TOKENS, D), jnp.float32)
    for choice_index in range(TOP):
        picked = outputs[chosen[:, choice_index]].astype(jnp.float32)
        mixed = mixed + gate_probs[:, choice_index][:, None] * picked
    return mixed.astype(jnp.bfloat16)
```

```python
import jax
import jax.numpy as jnp
from jax import lax
from jax.sharding import PartitionSpec as P


def swiglu_expert(rows, gate_part, up_part, down_part):
    gated = jnp.dot(rows, gate_part, preferred_element_type=jnp.float32)
    lifted = jnp.dot(rows, up_part, preferred_element_type=jnp.float32)
    hidden = (jax.nn.silu(gated) * lifted).astype(jnp.bfloat16)
    return jnp.dot(hidden, down_part, preferred_element_type=jnp.float32)


def slot_table(expert_ids, n_experts):
    routed = expert_ids.reshape(-1)
    pair_count = routed.shape[0]
    onehot = (routed[:, None] == jnp.arange(n_experts, dtype=jnp.int32)[None, :]).astype(
        jnp.bfloat16
    )
    row_index = lax.broadcasted_iota(jnp.int32, (pair_count, pair_count), 0)
    col_index = lax.broadcasted_iota(jnp.int32, (pair_count, pair_count), 1)
    earlier = (row_index > col_index).astype(jnp.bfloat16)
    before = jnp.dot(earlier, onehot, preferred_element_type=jnp.float32)
    slots = jnp.sum(before * onehot.astype(jnp.float32), axis=1).astype(jnp.int32)
    return (routed, slots)


def body(tokens, expert_ids, gate_probs, w_gate, w_up, w_down):
    n_experts = lax.axis_size("ep")
    tok_rows, top_count = expert_ids.shape
    capacity = 3 * tok_rows * top_count // (2 * n_experts)
    routed, slots = slot_table(expert_ids, n_experts)
    positions = routed * capacity + slots
    pair_token = jnp.repeat(jnp.arange(tok_rows, dtype=jnp.int32), top_count)
    buffer_rows = n_experts * capacity
    owners = jnp.full((buffer_rows,), tok_rows, jnp.int32).at[positions].set(pair_token)
    half_slots = capacity // 2
    whole_tokens = lax.all_gather(tokens, "tp", axis=1, tiled=True)
    width = whole_tokens.shape[1]
    gate_full, up_full = (
        lax.all_gather(w_gate, "tp", axis=2, tiled=True),
        lax.all_gather(w_up, "tp", axis=2, tiled=True),
    )
    down_full = lax.all_gather(w_down, "tp", axis=1, tiled=True)
    padded = jnp.concatenate([whole_tokens, jnp.zeros((1, width), whole_tokens.dtype)], 0)
    outgoing = padded[owners].reshape(n_experts, capacity, width)
    lane = lax.axis_index("tp")
    mine = lax.dynamic_slice_in_dim(outgoing, lane * half_slots, half_slots, 1)
    block = lax.all_to_all(mine, "ep", split_axis=0, concat_axis=0, tiled=True)
    sources, items, columns = block.shape
    result = swiglu_expert(
        block.reshape(sources * items, columns), gate_full[0], up_full[0], down_full[0]
    )
    result = result.astype(jnp.bfloat16).reshape(sources, items, columns)
    returned = lax.all_to_all(result, "ep", split_axis=0, concat_axis=0, tiled=True)
    received = returned.reshape(n_experts * half_slots, width)
    in_half = slots // half_slots == lane
    local_pos = routed * half_slots + slots % half_slots
    picked = received[local_pos].astype(jnp.float32).reshape(tok_rows, top_count, width)
    weighted = jnp.where(in_half.reshape(tok_rows, top_count), gate_probs, 0.0)
    partial_value = jnp.sum(weighted[:, :, None] * picked, axis=1)
    return lax.psum_scatter(partial_value, "tp", scatter_dimension=1, tiled=True).astype(
        jnp.bfloat16
    )


def dense_body(tokens, expert_ids, gate_probs, w_gate, w_up, w_down):
    n_experts = lax.axis_size("ep")
    tok_rows, _ = expert_ids.shape
    experts = jnp.arange(n_experts, dtype=jnp.int32)
    match = expert_ids[:, :, None] == experts[None, None, :]
    weight = jnp.sum(jnp.where(match, gate_probs[:, :, None], 0.0), axis=1)
    weights = lax.all_gather(weight, "ep", axis=0, tiled=True)
    mine = (experts == lax.axis_index("ep"))[None, :]
    column = jnp.sum(jnp.where(mine, weights, 0.0), axis=1, keepdims=True)
    rows = lax.all_gather(tokens, "tp", axis=1, tiled=True)
    rows = lax.all_gather(rows, "ep", axis=0, tiled=True)
    result = swiglu_expert(rows, w_gate[0], w_up[0], w_down[0]) * column
    result = lax.psum_scatter(result.astype(jnp.bfloat16), "tp", scatter_dimension=1, tiled=True)
    result = lax.psum_scatter(result, "ep", scatter_dimension=0, tiled=True)
    return result.astype(jnp.bfloat16)


def solution(mesh):
    in_specs = (
        P(("groups", "ep"), "tp"),
        P(("groups", "ep"), None),
        P(("groups", "ep"), None),
        P("ep", None, "tp"),
        P("ep", None, "tp"),
        P("ep", "tp", None),
    )
    out_specs = P(("groups", "ep"), "tp")

    def layer(tokens, expert_ids, gate_probs, w_gate, w_up, w_down):
        n_experts = lax.axis_size("ep")
        tok_rows, top_count = expert_ids.shape
        capacity = 3 * tok_rows * top_count // (2 * n_experts)
        chosen = dense_body if tok_rows <= 2 * capacity else body
        return chosen(tokens, expert_ids, gate_probs, w_gate, w_up, w_down)

    return jax.shard_map(layer, mesh=mesh, in_specs=in_specs, out_specs=out_specs, check_vma=False)
```

```python
import functools

import jax
import jax.numpy as jnp
from jax import lax
from jax.experimental import pallas as pl
from jax.experimental.pallas import tpu as pltpu
from jax.sharding import PartitionSpec as P


def swiglu_expert(rows, gate_part, up_part, down_part):
    gated = jnp.dot(rows, gate_part, preferred_element_type=jnp.float32)
    lifted = jnp.dot(rows, up_part, preferred_element_type=jnp.float32)
    hidden = (jax.nn.silu(gated) * lifted).astype(jnp.bfloat16)
    return jnp.dot(hidden, down_part, preferred_element_type=jnp.float32)


def slot_table(expert_ids, n_experts):
    routed = expert_ids.reshape(-1)
    pair_count = routed.shape[0]
    onehot = (routed[:, None] == jnp.arange(n_experts, dtype=jnp.int32)[None, :]).astype(
        jnp.bfloat16
    )
    row_index = lax.broadcasted_iota(jnp.int32, (pair_count, pair_count), 0)
    col_index = lax.broadcasted_iota(jnp.int32, (pair_count, pair_count), 1)
    earlier = (row_index > col_index).astype(jnp.bfloat16)
    before = jnp.dot(earlier, onehot, preferred_element_type=jnp.float32)
    slots = jnp.sum(before * onehot.astype(jnp.float32), axis=1).astype(jnp.int32)
    return (routed, slots)


def body(tokens, expert_ids, gate_probs, w_gate, w_up, w_down):
    n_experts = lax.axis_size("ep")
    tok_rows, top_count = expert_ids.shape
    capacity = 3 * tok_rows * top_count // (2 * n_experts)
    routed, slots = slot_table(expert_ids, n_experts)
    positions = routed * capacity + slots
    pair_token = jnp.repeat(jnp.arange(tok_rows, dtype=jnp.int32), top_count)
    buffer_rows = n_experts * capacity
    owners = jnp.full((buffer_rows,), tok_rows, jnp.int32).at[positions].set(pair_token)
    half_slots = capacity // 2
    whole_tokens = lax.all_gather(tokens, "tp", axis=1, tiled=True)
    width = whole_tokens.shape[1]
    gate_full, up_full = (
        lax.all_gather(w_gate, "tp", axis=2, tiled=True),
        lax.all_gather(w_up, "tp", axis=2, tiled=True),
    )
    down_full = lax.all_gather(w_down, "tp", axis=1, tiled=True)
    padded = jnp.concatenate([whole_tokens, jnp.zeros((1, width), whole_tokens.dtype)], 0)
    outgoing = padded[owners].reshape(n_experts, capacity, width)
    lane = lax.axis_index("tp")
    mine = lax.dynamic_slice_in_dim(outgoing, lane * half_slots, half_slots, 1)
    block = lax.all_to_all(mine, "ep", split_axis=0, concat_axis=0, tiled=True)
    sources, items, columns = block.shape
    result = swiglu_expert(
        block.reshape(sources * items, columns), gate_full[0], up_full[0], down_full[0]
    )
    result = result.astype(jnp.bfloat16).reshape(sources, items, columns)
    returned = lax.all_to_all(result, "ep", split_axis=0, concat_axis=0, tiled=True)
    received = returned.reshape(n_experts * half_slots, width)
    in_half = slots // half_slots == lane
    local_pos = routed * half_slots + slots % half_slots
    picked = received[local_pos].astype(jnp.float32).reshape(tok_rows, top_count, width)
    weighted = jnp.where(in_half.reshape(tok_rows, top_count), gate_probs, 0.0)
    partial_value = jnp.sum(weighted[:, :, None] * picked, axis=1)
    return lax.psum_scatter(partial_value, "tp", scatter_dimension=1, tiled=True).astype(
        jnp.bfloat16
    )


MESH = pl.DeviceIdType.MESH


def flip(position, step):
    low, high = step % 2, step // 2
    return position + low * (1 - 2 * (position % 2)) + high * (2 - 4 * ((position // 2) % 2))


def dense_kernel(
    n,
    tokens,
    ids,
    gates,
    w_gate,
    w_up,
    w_down,
    out,
    gathered,
    shares,
    gate_v,
    up_v,
    down_v,
    down_half,
    kept,
    core_out,
    core_in,
    side_out,
    side_in,
    line_out,
    line_in,
    total,
    load_sem,
    share_send,
    share_recv,
    line_send,
    line_recv,
    side_send,
    side_recv,
    core_send,
    core_recv,
    sum_core_send,
    sum_core_recv,
    sum_side_send,
    sum_side_recv,
    sum_line_send,
    sum_line_recv,
):
    group, me, lane = lax.axis_index("groups"), lax.axis_index("ep"), lax.axis_index("tp")
    line = n // 2
    row, side = me // 2, me % 2
    rows, half = tokens.shape
    ff = gate_v.shape[1]
    mate = (group, me, 1 - lane)
    across = (group, row * 2 + 1 - side, lane)

    def along(step):
        return (group, flip(row, step) * 2 + side, lane)

    def remote(src, dst, send, recv, device):
        return pltpu.make_async_remote_copy(
            src_ref=src, dst_ref=dst, send_sem=send, recv_sem=recv,
            device_id=device, device_id_type=MESH,
        )

    def mine(step):
        return flip(row, step) * 2 + side

    def theirs(step):
        return flip(row, step) * 2 + 1 - side

    def line_copy(step, block, device):
        ref = gathered.at[block, lane]
        return remote(ref, ref, line_send.at[step], line_recv.at[step], device)

    def side_copy(step, block):
        ref = gathered.at[block, lane]
        return remote(ref, ref, side_send.at[step], side_recv.at[step], across)

    def core_copy(step, which, block, which_half):
        ref = gathered.at[block, which_half]
        return remote(ref, ref, core_send.at[step, which], core_recv.at[step, which], mate)

    def share_copy(offset, block):
        ref = shares.at[block]
        device = (group, lax.rem(me + offset, n), lane)
        return remote(ref, ref, share_send.at[offset], share_recv.at[offset], device)

    own = pltpu.make_async_copy(tokens, gathered.at[me, lane], load_sem.at[3])
    own.start()
    loads = [
        pltpu.make_async_copy(w_gate.at[0], gate_v, load_sem.at[0]),
        pltpu.make_async_copy(w_up.at[0], up_v, load_sem.at[1]),
        pltpu.make_async_copy(w_down.at[0], down_v, load_sem.at[2]),
    ]

    barrier = pltpu.get_barrier_semaphore()
    for offset in range(1, n):
        pl.semaphore_signal(
            barrier, inc=1, device_id=(group, lax.rem(me + offset, n), lane), device_id_type=MESH
        )
    pl.semaphore_signal(barrier, inc=1, device_id=mate, device_id_type=MESH)

    width = shares.shape[2]
    experts = lax.broadcasted_iota(jnp.int32, (rows, width), 1)
    weight = jnp.zeros((rows, width), jnp.float32)
    for choice in range(ids.shape[1]):
        hit = ids[:, choice : choice + 1] == experts
        weight = weight + jnp.where(hit, gates[:, choice : choice + 1], 0.0)
    weight = jnp.concatenate([weight, jnp.zeros((width - rows, width), jnp.float32)], axis=0)
    shares[me] = weight.T[:n]

    own.wait()
    pl.semaphore_wait(barrier, n)
    core_copy(0, 0, me, lane).start()
    side_copy(0, me).start()
    for step in range(1, line):
        line_copy(step, me, along(step)).start()
    for offset in range(1, n):
        share_copy(offset, me).start()
    for load in loads:
        load.start()
    loads[2].wait()
    down_half[0] = down_v[:, :half]
    down_half[1] = down_v[:, half:]
    loads[0].wait()
    loads[1].wait()
    for offset in range(1, n):
        share_copy(offset, lax.rem(me + n - offset, n)).wait_recv()

    diagonal = lax.broadcasted_iota(jnp.int32, (rows, width), 0) == lax.broadcasted_iota(
        jnp.int32, (rows, width), 1
    )

    def share_column(block):
        spread = jnp.broadcast_to(shares[block, pl.ds(me, 1), :], (rows, width))
        return jnp.sum(jnp.where(diagonal, spread, 0.0), axis=1, keepdims=True)

    def forward(step):
        line_copy(step, mine(step), along(step)).wait_recv()
        side_copy(step, mine(step)).start()
        core_copy(step, 0, mine(step), lane).start()

    def expert(step):
        side_copy(step, theirs(step)).wait_recv()
        core_copy(step, 1, theirs(step), lane).start()
        core_copy(step, 0, mine(step), 1 - lane).wait_recv()
        core_copy(step, 1, theirs(step), 1 - lane).wait_recv()
        first = flip(row, step) * 2
        left = gathered[pl.ds(first, 2), 0].reshape(2 * rows, half)
        right = gathered[pl.ds(first, 2), 1].reshape(2 * rows, half)
        f32 = jnp.float32
        gated = jnp.dot(left, gate_v[:half, :], preferred_element_type=f32)
        gated = gated + jnp.dot(right, gate_v[half:, :], preferred_element_type=f32)
        lifted = jnp.dot(left, up_v[:half, :], preferred_element_type=f32)
        lifted = lifted + jnp.dot(right, up_v[half:, :], preferred_element_type=f32)
        hidden = (gated / (1.0 + jnp.exp(-gated)) * lifted).astype(jnp.bfloat16)
        column = jnp.concatenate([share_column(first), share_column(first + 1)], axis=0)
        away = jnp.dot(hidden, down_half[1 - lane], preferred_element_type=f32) * column
        core_out[step] = away.astype(jnp.bfloat16).reshape(2, rows, half)
        sum_core_copy(step).start()
        here = jnp.dot(hidden, down_half[lane], preferred_element_type=f32) * column
        kept[step] = here.reshape(2, rows, half)

    def sum_core_copy(step):
        return remote(
            core_out.at[step], core_in.at[step], sum_core_send.at[step], sum_core_recv.at[step], mate
        )

    def sum_side_copy(step):
        return remote(
            side_out.at[step], side_in.at[step], sum_side_send.at[step], sum_side_recv.at[step], across
        )

    def sum_line_copy(step):
        return remote(
            line_out.at[step], line_in.at[step], sum_line_send.at[step], sum_line_recv.at[step],
            along(step),
        )

    def join_cores(step):
        sum_core_copy(step).wait_recv()
        other = kept[step, 1 - side] + core_in[step, 1 - side].astype(jnp.float32)
        side_out[step] = other.astype(jnp.bfloat16)
        sum_side_copy(step).start()

    def join_sides(step):
        sum_side_copy(step).wait_recv()
        value = kept[step, side] + core_in[step, side].astype(jnp.float32)
        value = value + side_in[step].astype(jnp.float32)

        @pl.when(step == 0)
        def _():
            total[...] = value

        @pl.when(step > 0)
        def _():
            line_out[step] = value.astype(jnp.bfloat16)
            sum_line_copy(step).start()

    def iteration(turn, carry):
        @pl.when(turn + 1 < line)
        def _():
            forward(turn + 1)

        @pl.when((turn >= 1) & (turn <= line))
        def _():
            join_cores(turn - 1)

        @pl.when(turn < line)
        def _():
            expert(turn)

        @pl.when(turn >= 2)
        def _():
            join_sides(turn - 2)

        return carry

    lax.fori_loop(0, line + 2, iteration, 0)

    value = total[...]
    for step in range(1, line):
        sum_line_copy(step).wait_recv()
        value = value + line_in[step].astype(jnp.float32)
    out[...] = value.astype(jnp.bfloat16)

    for offset in range(1, n):
        share_copy(offset, me).wait_send()
    for step in range(line):
        side_copy(step, mine(step)).wait_send()
        core_copy(step, 0, mine(step), lane).wait_send()
        core_copy(step, 1, theirs(step), lane).wait_send()
        sum_core_copy(step).wait_send()
        sum_side_copy(step).wait_send()
        if step:
            line_copy(step, me, along(step)).wait_send()
            sum_line_copy(step).wait_send()


def dense_layer(tokens, expert_ids, gate_probs, w_gate, w_up, w_down):
    n = lax.axis_size("ep")
    line = n // 2
    rows, half = tokens.shape
    depth, ff = w_gate.shape[1:]
    bf16, f32 = jnp.bfloat16, jnp.float32
    vmem, anywhere = pl.BlockSpec(memory_space=pltpu.VMEM), pl.BlockSpec(memory_space=pl.ANY)
    dma = pltpu.SemaphoreType.DMA
    return pl.pallas_call(
        functools.partial(dense_kernel, n),
        out_shape=jax.ShapeDtypeStruct((rows, half), bf16),
        in_specs=[anywhere, vmem, vmem, anywhere, anywhere, anywhere],
        out_specs=vmem,
        scratch_shapes=[
            pltpu.VMEM((n, 2, rows, half), bf16),
            pltpu.VMEM((n, n, 128), f32),
            pltpu.VMEM((depth, ff), bf16),
            pltpu.VMEM((depth, ff), bf16),
            pltpu.VMEM((ff, depth), bf16),
            pltpu.VMEM((2, ff, half), bf16),
            pltpu.VMEM((line, 2, rows, half), f32),
            pltpu.VMEM((line, 2, rows, half), bf16),
            pltpu.VMEM((line, 2, rows, half), bf16),
            pltpu.VMEM((line, rows, half), bf16),
            pltpu.VMEM((line, rows, half), bf16),
            pltpu.VMEM((line, rows, half), bf16),
            pltpu.VMEM((line, rows, half), bf16),
            pltpu.VMEM((rows, half), f32),
            dma((4,)),
            dma((n,)),
            dma((n,)),
            dma((line,)),
            dma((line,)),
            dma((line,)),
            dma((line,)),
            dma((line, 2)),
            dma((line, 2)),
            dma((line,)),
            dma((line,)),
            dma((line,)),
            dma((line,)),
            dma((line,)),
            dma((line,)),
        ],
        compiler_params=pltpu.CompilerParams(
            collective_id=0, has_side_effects=True, vmem_limit_bytes=60000 * 1024
        ),
    )(tokens, expert_ids, gate_probs, w_gate, w_up, w_down)


def solution(mesh):
    in_specs = (
        P(("groups", "ep"), "tp"),
        P(("groups", "ep"), None),
        P(("groups", "ep"), None),
        P("ep", None, "tp"),
        P("ep", None, "tp"),
        P("ep", "tp", None),
    )
    out_specs = P(("groups", "ep"), "tp")

    def layer(tokens, expert_ids, gate_probs, w_gate, w_up, w_down):
        n_experts = lax.axis_size("ep")
        tok_rows, top_count = expert_ids.shape
        capacity = 3 * tok_rows * top_count // (2 * n_experts)
        dense = tok_rows <= 2 * capacity and n_experts == 8 and lax.axis_size("tp") == 2
        chosen = dense_layer if dense else body
        return chosen(tokens, expert_ids, gate_probs, w_gate, w_up, w_down)

    return jax.shard_map(layer, mesh=mesh, in_specs=in_specs, out_specs=out_specs, check_vma=False)
```

```python
import functools

import jax
import jax.numpy as jnp
from jax import lax
from jax.experimental import pallas as pl
from jax.experimental.pallas import tpu as pltpu
from jax.sharding import PartitionSpec as P


def swiglu_expert(rows, gate_part, up_part, down_part):
    gated = jnp.dot(rows, gate_part, preferred_element_type=jnp.float32)
    lifted = jnp.dot(rows, up_part, preferred_element_type=jnp.float32)
    hidden = (jax.nn.silu(gated) * lifted).astype(jnp.bfloat16)
    return jnp.dot(hidden, down_part, preferred_element_type=jnp.float32)


def slot_table(expert_ids, n_experts):
    routed = expert_ids.reshape(-1)
    pair_count = routed.shape[0]
    onehot = (routed[:, None] == jnp.arange(n_experts, dtype=jnp.int32)[None, :]).astype(
        jnp.bfloat16
    )
    row_index = lax.broadcasted_iota(jnp.int32, (pair_count, pair_count), 0)
    col_index = lax.broadcasted_iota(jnp.int32, (pair_count, pair_count), 1)
    earlier = (row_index > col_index).astype(jnp.bfloat16)
    before = jnp.dot(earlier, onehot, preferred_element_type=jnp.float32)
    slots = jnp.sum(before * onehot.astype(jnp.float32), axis=1).astype(jnp.int32)
    return (routed, slots)


def body(tokens, expert_ids, gate_probs, w_gate, w_up, w_down):
    n_experts = lax.axis_size("ep")
    tok_rows, top_count = expert_ids.shape
    capacity = 3 * tok_rows * top_count // (2 * n_experts)
    routed, slots = slot_table(expert_ids, n_experts)
    positions = routed * capacity + slots
    pair_token = jnp.repeat(jnp.arange(tok_rows, dtype=jnp.int32), top_count)
    buffer_rows = n_experts * capacity
    owners = jnp.full((buffer_rows,), tok_rows, jnp.int32).at[positions].set(pair_token)
    half_slots = capacity // 2
    whole_tokens = lax.all_gather(tokens, "tp", axis=1, tiled=True)
    width = whole_tokens.shape[1]
    gate_full, up_full = (
        lax.all_gather(w_gate, "tp", axis=2, tiled=True),
        lax.all_gather(w_up, "tp", axis=2, tiled=True),
    )
    down_full = lax.all_gather(w_down, "tp", axis=1, tiled=True)
    padded = jnp.concatenate([whole_tokens, jnp.zeros((1, width), whole_tokens.dtype)], 0)
    outgoing = padded[owners].reshape(n_experts, capacity, width)
    lane = lax.axis_index("tp")
    mine = lax.dynamic_slice_in_dim(outgoing, lane * half_slots, half_slots, 1)
    block = lax.all_to_all(mine, "ep", split_axis=0, concat_axis=0, tiled=True)
    sources, items, columns = block.shape
    result = swiglu_expert(
        block.reshape(sources * items, columns), gate_full[0], up_full[0], down_full[0]
    )
    result = result.astype(jnp.bfloat16).reshape(sources, items, columns)
    returned = lax.all_to_all(result, "ep", split_axis=0, concat_axis=0, tiled=True)
    received = returned.reshape(n_experts * half_slots, width)
    in_half = slots // half_slots == lane
    local_pos = routed * half_slots + slots % half_slots
    picked = received[local_pos].astype(jnp.float32).reshape(tok_rows, top_count, width)
    weighted = jnp.where(in_half.reshape(tok_rows, top_count), gate_probs, 0.0)
    partial_value = jnp.sum(weighted[:, :, None] * picked, axis=1)
    return lax.psum_scatter(partial_value, "tp", scatter_dimension=1, tiled=True).astype(
        jnp.bfloat16
    )


MESH = pl.DeviceIdType.MESH


def flip(position, step):
    low, high = step % 2, step // 2
    return position + low * (1 - 2 * (position % 2)) + high * (2 - 4 * ((position // 2) % 2))


def dense_kernel(
    n,
    tokens,
    ids,
    gates,
    w_gate,
    w_up,
    w_down,
    out,
    gathered,
    shares,
    gate_v,
    up_v,
    down_v,
    kept,
    core_out,
    core_in,
    side_out,
    side_in,
    line_out,
    line_in,
    total,
    load_sem,
    share_send,
    share_recv,
    line_send,
    line_recv,
    side_send,
    side_recv,
    core_send,
    core_recv,
    sum_core_send,
    sum_core_recv,
    sum_side_send,
    sum_side_recv,
    sum_line_send,
    sum_line_recv,
):
    group, me, lane = lax.axis_index("groups"), lax.axis_index("ep"), lax.axis_index("tp")
    line = n // 2
    row, side = me // 2, me % 2
    rows, half = tokens.shape
    mate = (group, me, 1 - lane)
    across = (group, row * 2 + 1 - side, lane)

    def along(step):
        return (group, flip(row, step) * 2 + side, lane)

    def remote(src, dst, send, recv, device):
        return pltpu.make_async_remote_copy(
            src_ref=src, dst_ref=dst, send_sem=send, recv_sem=recv,
            device_id=device, device_id_type=MESH,
        )

    def mine(step):
        return flip(row, step) * 2 + side

    def theirs(step):
        return flip(row, step) * 2 + 1 - side

    def line_copy(step, block, device):
        ref = gathered.at[block, lane]
        return remote(ref, ref, line_send.at[step], line_recv.at[step], device)

    def side_copy(step, block):
        ref = gathered.at[block, lane]
        return remote(ref, ref, side_send.at[step], side_recv.at[step], across)

    def core_copy(step, which, block, which_half):
        ref = gathered.at[block, which_half]
        return remote(ref, ref, core_send.at[step, which], core_recv.at[step, which], mate)

    def share_copy(offset, block):
        ref = shares.at[block]
        device = (group, lax.rem(me + offset, n), lane)
        return remote(ref, ref, share_send.at[offset], share_recv.at[offset], device)

    own = pltpu.make_async_copy(tokens, gathered.at[me, lane], load_sem.at[3])
    own.start()
    loads = [
        pltpu.make_async_copy(w_gate.at[0], gate_v, load_sem.at[0]),
        pltpu.make_async_copy(w_up.at[0], up_v, load_sem.at[1]),
        pltpu.make_async_copy(w_down.at[0], down_v, load_sem.at[2]),
    ]

    barrier = pltpu.get_barrier_semaphore()
    for offset in range(1, n):
        pl.semaphore_signal(
            barrier, inc=1, device_id=(group, lax.rem(me + offset, n), lane), device_id_type=MESH
        )
    pl.semaphore_signal(barrier, inc=1, device_id=mate, device_id_type=MESH)

    experts = lax.broadcasted_iota(jnp.int32, (n, rows), 0)
    weight = jnp.zeros((n, rows), jnp.float32)
    for choice in range(ids.shape[0]):
        hit = ids[choice : choice + 1, :] == experts
        weight = weight + jnp.where(hit, gates[choice : choice + 1, :], 0.0)
    shares[me] = weight

    own.wait()
    pl.semaphore_wait(barrier, n)
    core_copy(0, 0, me, lane).start()
    side_copy(0, me).start()
    for step in range(1, line):
        line_copy(step, me, along(step)).start()
    for offset in range(1, n):
        share_copy(offset, me).start()
    for load in loads:
        load.start()
    for load in loads:
        load.wait()
    for offset in range(1, n):
        share_copy(offset, lax.rem(me + n - offset, n)).wait_recv()

    diagonal = lax.broadcasted_iota(jnp.int32, (rows, rows), 0) == lax.broadcasted_iota(
        jnp.int32, (rows, rows), 1
    )

    def share_column(block):
        spread = jnp.broadcast_to(shares[block, pl.ds(me, 1), :], (rows, rows))
        return jnp.sum(jnp.where(diagonal, spread, 0.0), axis=1, keepdims=True)

    def forward(step):
        line_copy(step, mine(step), along(step)).wait_recv()
        side_copy(step, mine(step)).start()
        core_copy(step, 0, mine(step), lane).start()

    def expert(step):
        side_copy(step, theirs(step)).wait_recv()
        core_copy(step, 1, theirs(step), lane).start()
        core_copy(step, 0, mine(step), 1 - lane).wait_recv()
        core_copy(step, 1, theirs(step), 1 - lane).wait_recv()
        first = flip(row, step) * 2
        left = gathered[pl.ds(first, 2), 0].reshape(2 * rows, half)
        right = gathered[pl.ds(first, 2), 1].reshape(2 * rows, half)
        whole = jnp.concatenate([left, right], axis=1)
        f32 = jnp.float32
        last = (((1,), (1,)), ((), ()))
        gated = lax.dot_general(whole, gate_v[...], last, preferred_element_type=f32)
        lifted = lax.dot_general(whole, up_v[...], last, preferred_element_type=f32)
        hidden = (gated / (1.0 + jnp.exp(-gated)) * lifted).astype(jnp.bfloat16)
        column = jnp.concatenate([share_column(first), share_column(first + 1)], axis=0)
        result = jnp.dot(hidden, down_v[...], preferred_element_type=f32) * column

        def split(away, here):
            core_out[step] = away.astype(jnp.bfloat16).reshape(2, rows, half)
            sum_core_copy(step).start()
            kept[step] = here.reshape(2, rows, half)

        @pl.when(lane == 0)
        def _():
            split(result[:, half:], result[:, :half])

        @pl.when(lane == 1)
        def _():
            split(result[:, :half], result[:, half:])

    def sum_core_copy(step):
        return remote(
            core_out.at[step], core_in.at[step], sum_core_send.at[step], sum_core_recv.at[step], mate
        )

    def sum_side_copy(step):
        return remote(
            side_out.at[step], side_in.at[step], sum_side_send.at[step], sum_side_recv.at[step], across
        )

    def sum_line_copy(step):
        return remote(
            line_out.at[step], line_in.at[step], sum_line_send.at[step], sum_line_recv.at[step],
            along(step),
        )

    def join_cores(step):
        sum_core_copy(step).wait_recv()
        other = kept[step, 1 - side] + core_in[step, 1 - side].astype(jnp.float32)
        side_out[step] = other.astype(jnp.bfloat16)
        sum_side_copy(step).start()

    def join_sides(step):
        sum_side_copy(step).wait_recv()
        value = kept[step, side] + core_in[step, side].astype(jnp.float32)
        value = value + side_in[step].astype(jnp.float32)

        @pl.when(step == 0)
        def _():
            total[...] = value

        @pl.when(step > 0)
        def _():
            line_out[step] = value.astype(jnp.bfloat16)
            sum_line_copy(step).start()

    def iteration(turn, carry):
        @pl.when(turn + 1 < line)
        def _():
            forward(turn + 1)

        @pl.when((turn >= 1) & (turn <= line))
        def _():
            join_cores(turn - 1)

        @pl.when(turn < line)
        def _():
            expert(turn)

        @pl.when(turn >= 2)
        def _():
            join_sides(turn - 2)

        return carry

    lax.fori_loop(0, line + 2, iteration, 0)

    value = total[...]
    for step in range(1, line):
        sum_line_copy(step).wait_recv()
        value = value + line_in[step].astype(jnp.float32)
    out[...] = value.astype(jnp.bfloat16)

    for offset in range(1, n):
        share_copy(offset, me).wait_send()
    for step in range(line):
        side_copy(step, mine(step)).wait_send()
        core_copy(step, 0, mine(step), lane).wait_send()
        core_copy(step, 1, theirs(step), lane).wait_send()
        sum_core_copy(step).wait_send()
        sum_side_copy(step).wait_send()
        if step:
            line_copy(step, me, along(step)).wait_send()
            sum_line_copy(step).wait_send()


def dense_layer(tokens, expert_ids, gate_probs, w_gate, w_up, w_down):
    n = lax.axis_size("ep")
    line = n // 2
    rows, half = tokens.shape
    depth, ff = w_gate.shape[1:]
    bf16, f32 = jnp.bfloat16, jnp.float32
    vmem, anywhere = pl.BlockSpec(memory_space=pltpu.VMEM), pl.BlockSpec(memory_space=pl.ANY)
    dma = pltpu.SemaphoreType.DMA
    return pl.pallas_call(
        functools.partial(dense_kernel, n),
        out_shape=jax.ShapeDtypeStruct((rows, half), bf16),
        in_specs=[anywhere, vmem, vmem, anywhere, anywhere, anywhere],
        out_specs=vmem,
        scratch_shapes=[
            pltpu.VMEM((n, 2, rows, half), bf16),
            pltpu.VMEM((n, n, rows), f32),
            pltpu.VMEM((ff, depth), bf16),
            pltpu.VMEM((ff, depth), bf16),
            pltpu.VMEM((ff, depth), bf16),
            pltpu.VMEM((line, 2, rows, half), f32),
            pltpu.VMEM((line, 2, rows, half), bf16),
            pltpu.VMEM((line, 2, rows, half), bf16),
            pltpu.VMEM((line, rows, half), bf16),
            pltpu.VMEM((line, rows, half), bf16),
            pltpu.VMEM((line, rows, half), bf16),
            pltpu.VMEM((line, rows, half), bf16),
            pltpu.VMEM((rows, half), f32),
            dma((4,)),
            dma((n,)),
            dma((n,)),
            dma((line,)),
            dma((line,)),
            dma((line,)),
            dma((line,)),
            dma((line, 2)),
            dma((line, 2)),
            dma((line,)),
            dma((line,)),
            dma((line,)),
            dma((line,)),
            dma((line,)),
            dma((line,)),
        ],
        compiler_params=pltpu.CompilerParams(
            collective_id=0, has_side_effects=True, vmem_limit_bytes=60000 * 1024
        ),
    )(
        tokens,
        expert_ids.T,
        gate_probs.T,
        jnp.swapaxes(w_gate, 1, 2),
        jnp.swapaxes(w_up, 1, 2),
        w_down,
    )


def solution(mesh):
    in_specs = (
        P(("groups", "ep"), "tp"),
        P(("groups", "ep"), None),
        P(("groups", "ep"), None),
        P("ep", None, "tp"),
        P("ep", None, "tp"),
        P("ep", "tp", None),
    )
    out_specs = P(("groups", "ep"), "tp")

    def layer(tokens, expert_ids, gate_probs, w_gate, w_up, w_down):
        n_experts = lax.axis_size("ep")
        tok_rows, top_count = expert_ids.shape
        capacity = 3 * tok_rows * top_count // (2 * n_experts)
        dense = tok_rows <= 2 * capacity and n_experts == 8 and lax.axis_size("tp") == 2
        chosen = dense_layer if dense else body
        return chosen(tokens, expert_ids, gate_probs, w_gate, w_up, w_down)

    return jax.shard_map(layer, mesh=mesh, in_specs=in_specs, out_specs=out_specs, check_vma=False)
```

```python
import functools

import jax
import jax.numpy as jnp
from jax import lax
from jax.experimental import pallas as pl
from jax.experimental.pallas import tpu as pltpu
from jax.sharding import PartitionSpec as P


def swiglu_expert(rows, gate_part, up_part, down_part):
    gated = jnp.dot(rows, gate_part, preferred_element_type=jnp.float32)
    lifted = jnp.dot(rows, up_part, preferred_element_type=jnp.float32)
    hidden = (jax.nn.silu(gated) * lifted).astype(jnp.bfloat16)
    return jnp.dot(hidden, down_part, preferred_element_type=jnp.float32)


def slot_table(expert_ids, n_experts):
    routed = expert_ids.reshape(-1)
    pair_count = routed.shape[0]
    onehot = (routed[:, None] == jnp.arange(n_experts, dtype=jnp.int32)[None, :]).astype(
        jnp.bfloat16
    )
    row_index = lax.broadcasted_iota(jnp.int32, (pair_count, pair_count), 0)
    col_index = lax.broadcasted_iota(jnp.int32, (pair_count, pair_count), 1)
    earlier = (row_index > col_index).astype(jnp.bfloat16)
    before = jnp.dot(earlier, onehot, preferred_element_type=jnp.float32)
    slots = jnp.sum(before * onehot.astype(jnp.float32), axis=1).astype(jnp.int32)
    return (routed, slots)


def body(tokens, expert_ids, gate_probs, w_gate, w_up, w_down):
    n_experts = lax.axis_size("ep")
    tok_rows, top_count = expert_ids.shape
    capacity = 3 * tok_rows * top_count // (2 * n_experts)
    routed, slots = slot_table(expert_ids, n_experts)
    positions = routed * capacity + slots
    pair_token = jnp.repeat(jnp.arange(tok_rows, dtype=jnp.int32), top_count)
    buffer_rows = n_experts * capacity
    owners = jnp.full((buffer_rows,), tok_rows, jnp.int32).at[positions].set(pair_token)
    half_slots = capacity // 2
    whole_tokens = lax.all_gather(tokens, "tp", axis=1, tiled=True)
    width = whole_tokens.shape[1]
    gate_full, up_full = (
        lax.all_gather(w_gate, "tp", axis=2, tiled=True),
        lax.all_gather(w_up, "tp", axis=2, tiled=True),
    )
    down_full = lax.all_gather(w_down, "tp", axis=1, tiled=True)
    padded = jnp.concatenate([whole_tokens, jnp.zeros((1, width), whole_tokens.dtype)], 0)
    outgoing = padded[owners].reshape(n_experts, capacity, width)
    lane = lax.axis_index("tp")
    mine = lax.dynamic_slice_in_dim(outgoing, lane * half_slots, half_slots, 1)
    block = lax.all_to_all(mine, "ep", split_axis=0, concat_axis=0, tiled=True)
    sources, items, columns = block.shape
    result = swiglu_expert(
        block.reshape(sources * items, columns), gate_full[0], up_full[0], down_full[0]
    )
    result = result.astype(jnp.bfloat16).reshape(sources, items, columns)
    returned = lax.all_to_all(result, "ep", split_axis=0, concat_axis=0, tiled=True)
    received = returned.reshape(n_experts * half_slots, width)
    in_half = slots // half_slots == lane
    local_pos = routed * half_slots + slots % half_slots
    picked = received[local_pos].astype(jnp.float32).reshape(tok_rows, top_count, width)
    weighted = jnp.where(in_half.reshape(tok_rows, top_count), gate_probs, 0.0)
    partial_value = jnp.sum(weighted[:, :, None] * picked, axis=1)
    return lax.psum_scatter(partial_value, "tp", scatter_dimension=1, tiled=True).astype(
        jnp.bfloat16
    )


MESH = pl.DeviceIdType.MESH


def flip(position, step):
    low, high = step % 2, step // 2
    return position + low * (1 - 2 * (position % 2)) + high * (2 - 4 * ((position // 2) % 2))


def dense_kernel(
    n,
    tokens,
    ids,
    gates,
    w_gate,
    w_up,
    w_down,
    out,
    gathered,
    tok_out,
    tok_in,
    shares,
    gate_v,
    up_v,
    down_v,
    kept,
    core_out,
    core_in,
    side_out,
    side_in,
    line_out,
    line_in,
    total,
    load_sem,
    share_send,
    share_recv,
    line_send,
    line_recv,
    side_send,
    side_recv,
    core_send,
    core_recv,
    sum_core_send,
    sum_core_recv,
    sum_side_send,
    sum_side_recv,
    sum_line_send,
    sum_line_recv,
):
    group, me, lane = lax.axis_index("groups"), lax.axis_index("ep"), lax.axis_index("tp")
    line = n // 2
    row, side = me // 2, me % 2
    rows, half = tokens.shape
    cap = tok_out.shape[1]
    other_expert = row * 2 + 1 - side
    mate = (group, me, 1 - lane)
    across = (group, row * 2 + 1 - side, lane)

    def along(step):
        return (group, flip(row, step) * 2 + side, lane)

    def remote(src, dst, send, recv, device):
        return pltpu.make_async_remote_copy(
            src_ref=src, dst_ref=dst, send_sem=send, recv_sem=recv,
            device_id=device, device_id_type=MESH,
        )

    def mine(step):
        return flip(row, step) * 2 + side

    def theirs(step):
        return flip(row, step) * 2 + 1 - side

    def line_copy(step, block, device):
        ref = gathered.at[block, lane]
        return remote(ref, ref, line_send.at[step], line_recv.at[step], device)

    def side_copy(step, block):
        return remote(
            tok_out.at[step], tok_in.at[step, lane], side_send.at[step], side_recv.at[step], across
        )

    def core_copy(step, which, block, which_half):
        ref = tok_in.at[step, which_half] if which else gathered.at[block, which_half]
        return remote(ref, ref, core_send.at[step, which], core_recv.at[step, which], mate)

    def share_row(block, expert, count):
        return jnp.broadcast_to(shares[block, pl.ds(expert, 1), :], (count, rows))

    def picker(block, expert):
        hit = share_row(block, expert, cap) > 0.0
        upper = lax.broadcasted_iota(jnp.int32, (rows, rows), 0) < lax.broadcasted_iota(
            jnp.int32, (rows, rows), 1
        )
        before = jnp.dot(
            jnp.where(hit, 1.0, 0.0).astype(jnp.bfloat16),
            jnp.where(upper, 1.0, 0.0).astype(jnp.bfloat16),
            preferred_element_type=jnp.float32,
        )
        slot = lax.broadcasted_iota(jnp.int32, (cap, rows), 0).astype(jnp.float32)
        return jnp.where(hit & (before == slot), 1.0, 0.0)

    def pack(step, block):
        chosen = picker(block, other_expert).astype(jnp.bfloat16)
        moved = jnp.dot(chosen, gathered[block, lane], preferred_element_type=jnp.float32)
        tok_out[step] = moved.astype(jnp.bfloat16)

    def share_copy(offset, block):
        ref = shares.at[block]
        device = (group, lax.rem(me + offset, n), lane)
        return remote(ref, ref, share_send.at[offset], share_recv.at[offset], device)

    own = pltpu.make_async_copy(tokens, gathered.at[me, lane], load_sem.at[3])
    own.start()
    loads = [
        pltpu.make_async_copy(w_gate.at[0], gate_v, load_sem.at[0]),
        pltpu.make_async_copy(w_up.at[0], up_v, load_sem.at[1]),
        pltpu.make_async_copy(w_down.at[0], down_v, load_sem.at[2]),
    ]

    barrier = pltpu.get_barrier_semaphore()
    for offset in range(1, n):
        pl.semaphore_signal(
            barrier, inc=1, device_id=(group, lax.rem(me + offset, n), lane), device_id_type=MESH
        )
    pl.semaphore_signal(barrier, inc=1, device_id=mate, device_id_type=MESH)

    experts = lax.broadcasted_iota(jnp.int32, (n, rows), 0)
    weight = jnp.zeros((n, rows), jnp.float32)
    for choice in range(ids.shape[0]):
        hit = ids[choice : choice + 1, :] == experts
        weight = weight + jnp.where(hit, gates[choice : choice + 1, :], 0.0)
    shares[me] = weight

    own.wait()
    pack(0, me)
    pl.semaphore_wait(barrier, n)
    core_copy(0, 0, me, lane).start()
    side_copy(0, me).start()
    for step in range(1, line):
        line_copy(step, me, along(step)).start()
    for offset in range(1, n):
        share_copy(offset, me).start()
    for load in loads:
        load.start()
    for load in loads:
        load.wait()
    for offset in range(1, n):
        share_copy(offset, lax.rem(me + n - offset, n)).wait_recv()

    diagonal = lax.broadcasted_iota(jnp.int32, (rows, rows), 0) == lax.broadcasted_iota(
        jnp.int32, (rows, rows), 1
    )

    def share_column(block):
        spread = jnp.broadcast_to(shares[block, pl.ds(me, 1), :], (rows, rows))
        return jnp.sum(jnp.where(diagonal, spread, 0.0), axis=1, keepdims=True)

    def forward(step):
        line_copy(step, mine(step), along(step)).wait_recv()
        pack(step, mine(step))
        side_copy(step, mine(step)).start()
        core_copy(step, 0, mine(step), lane).start()

    def expert(step):
        side_copy(step, theirs(step)).wait_recv()
        core_copy(step, 1, theirs(step), lane).start()
        core_copy(step, 0, mine(step), 1 - lane).wait_recv()
        core_copy(step, 1, theirs(step), 1 - lane).wait_recv()
        left = jnp.concatenate([gathered[mine(step), 0], tok_in[step, 0]], axis=0)
        right = jnp.concatenate([gathered[mine(step), 1], tok_in[step, 1]], axis=0)
        whole = jnp.concatenate([left, right], axis=1)
        f32 = jnp.float32
        last = (((1,), (1,)), ((), ()))
        gated = lax.dot_general(whole, gate_v[...], last, preferred_element_type=f32)
        lifted = lax.dot_general(whole, up_v[...], last, preferred_element_type=f32)
        hidden = (gated / (1.0 + jnp.exp(-gated)) * lifted).astype(jnp.bfloat16)
        packed = picker(theirs(step), me) * share_row(theirs(step), me, cap)
        packed = jnp.sum(packed, axis=1, keepdims=True)
        column = jnp.concatenate([share_column(mine(step)), packed], axis=0)
        result = jnp.dot(hidden, down_v[...], preferred_element_type=f32) * column

        def split(away, here):
            core_out[step] = away.astype(jnp.bfloat16)
            sum_core_copy(step).start()
            kept[step] = here

        @pl.when(lane == 0)
        def _():
            split(result[:, half:], result[:, :half])

        @pl.when(lane == 1)
        def _():
            split(result[:, :half], result[:, half:])

    def sum_core_copy(step):
        return remote(
            core_out.at[step], core_in.at[step], sum_core_send.at[step], sum_core_recv.at[step], mate
        )

    def sum_side_copy(step):
        return remote(
            side_out.at[step], side_in.at[step], sum_side_send.at[step], sum_side_recv.at[step], across
        )

    def sum_line_copy(step):
        return remote(
            line_out.at[step], line_in.at[step], sum_line_send.at[step], sum_line_recv.at[step],
            along(step),
        )

    def join_cores(step):
        sum_core_copy(step).wait_recv()
        other = kept[step, rows:] + core_in[step, rows:].astype(jnp.float32)
        side_out[step] = other.astype(jnp.bfloat16)
        sum_side_copy(step).start()

    def join_sides(step):
        sum_side_copy(step).wait_recv()
        value = kept[step, :rows] + core_in[step, :rows].astype(jnp.float32)
        chosen = picker(mine(step), other_expert).astype(jnp.bfloat16)
        spread = (((0,), (0,)), ((), ()))
        value = value + lax.dot_general(
            chosen, side_in[step], spread, preferred_element_type=jnp.float32
        )

        @pl.when(step == 0)
        def _():
            total[...] = value

        @pl.when(step > 0)
        def _():
            line_out[step] = value.astype(jnp.bfloat16)
            sum_line_copy(step).start()

    def iteration(turn, carry):
        @pl.when(turn + 1 < line)
        def _():
            forward(turn + 1)

        @pl.when((turn >= 1) & (turn <= line))
        def _():
            join_cores(turn - 1)

        @pl.when(turn < line)
        def _():
            expert(turn)

        @pl.when(turn >= 2)
        def _():
            join_sides(turn - 2)

        return carry

    lax.fori_loop(0, line + 2, iteration, 0)

    value = total[...]
    for step in range(1, line):
        sum_line_copy(step).wait_recv()
        value = value + line_in[step].astype(jnp.float32)
    out[...] = value.astype(jnp.bfloat16)

    for offset in range(1, n):
        share_copy(offset, me).wait_send()
    for step in range(line):
        side_copy(step, mine(step)).wait_send()
        core_copy(step, 0, mine(step), lane).wait_send()
        core_copy(step, 1, theirs(step), lane).wait_send()
        sum_core_copy(step).wait_send()
        sum_side_copy(step).wait_send()
        if step:
            line_copy(step, me, along(step)).wait_send()
            sum_line_copy(step).wait_send()


def dense_layer(tokens, expert_ids, gate_probs, w_gate, w_up, w_down):
    n = lax.axis_size("ep")
    line = n // 2
    rows, half = tokens.shape
    depth, ff = w_gate.shape[1:]
    cap = 3 * rows * expert_ids.shape[1] // (2 * n)
    bf16, f32 = jnp.bfloat16, jnp.float32
    vmem, anywhere = pl.BlockSpec(memory_space=pltpu.VMEM), pl.BlockSpec(memory_space=pl.ANY)
    dma = pltpu.SemaphoreType.DMA
    return pl.pallas_call(
        functools.partial(dense_kernel, n),
        out_shape=jax.ShapeDtypeStruct((rows, half), bf16),
        in_specs=[anywhere, vmem, vmem, anywhere, anywhere, anywhere],
        out_specs=vmem,
        scratch_shapes=[
            pltpu.VMEM((n, 2, rows, half), bf16),
            pltpu.VMEM((line, cap, half), bf16),
            pltpu.VMEM((line, 2, cap, half), bf16),
            pltpu.VMEM((n, n, rows), f32),
            pltpu.VMEM((ff, depth), bf16),
            pltpu.VMEM((ff, depth), bf16),
            pltpu.VMEM((ff, depth), bf16),
            pltpu.VMEM((line, rows + cap, half), f32),
            pltpu.VMEM((line, rows + cap, half), bf16),
            pltpu.VMEM((line, rows + cap, half), bf16),
            pltpu.VMEM((line, cap, half), bf16),
            pltpu.VMEM((line, cap, half), bf16),
            pltpu.VMEM((line, rows, half), bf16),
            pltpu.VMEM((line, rows, half), bf16),
            pltpu.VMEM((rows, half), f32),
            dma((4,)),
            dma((n,)),
            dma((n,)),
            dma((line,)),
            dma((line,)),
            dma((line,)),
            dma((line,)),
            dma((line, 2)),
            dma((line, 2)),
            dma((line,)),
            dma((line,)),
            dma((line,)),
            dma((line,)),
            dma((line,)),
            dma((line,)),
        ],
        compiler_params=pltpu.CompilerParams(
            collective_id=0, has_side_effects=True, vmem_limit_bytes=60000 * 1024
        ),
    )(
        tokens,
        expert_ids.T,
        gate_probs.T,
        jnp.swapaxes(w_gate, 1, 2),
        jnp.swapaxes(w_up, 1, 2),
        w_down,
    )


def solution(mesh):
    in_specs = (
        P(("groups", "ep"), "tp"),
        P(("groups", "ep"), None),
        P(("groups", "ep"), None),
        P("ep", None, "tp"),
        P("ep", None, "tp"),
        P("ep", "tp", None),
    )
    out_specs = P(("groups", "ep"), "tp")

    def layer(tokens, expert_ids, gate_probs, w_gate, w_up, w_down):
        n_experts = lax.axis_size("ep")
        tok_rows, top_count = expert_ids.shape
        capacity = 3 * tok_rows * top_count // (2 * n_experts)
        dense = tok_rows <= 2 * capacity and n_experts == 8 and lax.axis_size("tp") == 2
        chosen = dense_layer if dense else body
        return chosen(tokens, expert_ids, gate_probs, w_gate, w_up, w_down)

    return jax.shard_map(layer, mesh=mesh, in_specs=in_specs, out_specs=out_specs, check_vma=False)
```
